256 devices in a mesh: row: 16 (over z_hi, y), col: 16 (over z_lo, x, core).
Axes of the slice: x: 4, y: 4, z: 8 (z_hi: 4, z_lo: 2; z = z_hi * 2 + z_lo), core: 2. Of those that a mesh axis runs over, the one named last changes fastest.
Arguments:
- interaction: bfloat16 [8192, 8192], P('row', 'col'), may hold values from -0.0625 to 0.0625
- amplitudes: bfloat16 [8192, 8192], P('row', 'col'), may hold values from -6 to 6
- driver: bfloat16 [8192, 8192], P('row', 'col'), may hold values from -6 to 6
- dressing: bfloat16 [1024, 1024], replicated, may hold values from -0.1875 to 0.1875
- occ_energy: float32 [8], replicated, may hold values from -2 to -0.5
- vir_energy: float32 [1024], replicated, may hold values from 0.5 to 3
Outputs:
- updated: float32 [8192, 8192], P('row', 'col')
The draws below stay inside these ranges and needn't reach their ends.
All inputs are finite; a program needn't handle non-finite values.
Results may differ from the reference program's by a relative error of at most 0.00084.
Values may be sent and summed in bfloat16 or wider, within the bound.
No kernel may reach another device: no remote copies, remote signals or barrier semaphores. Data moves between devices by JAX's collectives and lax.ppermute only.
A program may use at most 64 MiB of HBM per device.

```python
import jax
import jax.numpy as jnp

V = 1024
OCC = 8
K = 8192
ROWS = 8192
COLUMNS = 8192


def level_of(stream_key, dims, cuts, low, top_value):
    loudness, own = 1.0, jax.random.fold_in(stream_key, 6)
    for position, parts in cuts:
        heights = jnp.exp(jax.random.uniform(jax.random.fold_in(own, position), (parts,), jnp.float32, low / len(cuts), top_value / len(cuts)))
        loudness = loudness * jnp.repeat(heights, dims[position] // parts).reshape([-1 if axis == position else 1 for axis in range(len(dims))])
    return loudness


def centred(key, dims, deviation, reach, shards=(), kind=jnp.bfloat16):
    entries = deviation * jax.random.normal(key, dims, jnp.float32)
    if shards:
        entries = entries * level_of(key, dims, shards, -0.22, 0.18)
    return jnp.clip(entries, -reach, reach).astype(kind)


def setup_inputs(seed: int = 0) -> dict:
    keys = jax.random.split(jax.random.key(seed), 7)
    interaction = centred(keys[0], (ROWS, K), K ** -0.5, 0.0625, ((0, 16), (1, 16)))
    amplitudes = centred(keys[1], (K, COLUMNS), 1.0, 6.0, ((0, 16), (1, 16)))
    driver = centred(keys[2], (ROWS, COLUMNS), 1.0, 6.0, ((0, 16), (1, 16)))
    dressing = centred(keys[3], (V, V), V ** -0.5, 0.1875)
    occ_energy = jnp.clip(jax.random.uniform(keys[4], (OCC,), jnp.float32, -2.0, -0.5), -2.0, -0.5)
    vir_energy = jnp.clip(jax.random.uniform(keys[5], (V,), jnp.float32, 0.5, 3.0), 0.5, 3.0)
    return dict(interaction=interaction, amplitudes=amplitudes, driver=driver, dressing=dressing, occ_energy=occ_energy, vir_energy=vir_energy)


def reference(interaction, amplitudes, driver, dressing, occ_energy, vir_energy):
    cycle_term = jnp.dot(interaction, amplitudes, preferred_element_type=jnp.float32)
    line_energy = jnp.repeat(occ_energy, V) - jnp.tile(vir_energy, OCC)
    denominator = line_energy[:, None] + line_energy[None, :]
    summed = driver.astype(jnp.float32) + cycle_term
    first_order = (summed / denominator).astype(jnp.bfloat16)
    flattened = first_order.reshape(ROWS * OCC, V)
    dressed = jnp.dot(flattened, dressing, preferred_element_type=jnp.float32)
    dressed = dressed.reshape(ROWS, COLUMNS).astype(jnp.bfloat16)
    return (summed + dressed.astype(jnp.float32)) / denominator
```

```python
import jax
import jax.numpy as jnp
from jax import lax
from jax.sharding import PartitionSpec as P

AXES = ("row", "col")


def device_index(x, y, high, low, core):
    return ((high % 4) * 4 + y % 4) * 16 + (low % 2) * 8 + (x % 4) * 2 + core % 2


def moved(dx=0, dy=0, high=0, low=0, core=0):
    pairs = []
    for x in range(4):
        for y in range(4):
            for zh in range(4):
                for zl in range(2):
                    for k in range(2):
                        pairs.append(
                            (
                                device_index(x, y, zh, zl, k),
                                device_index(x + dx, y + dy, zh + high, zl + low, k + core),
                            )
                        )
    return pairs


def send(block, **by):
    return lax.ppermute(block, AXES, moved(**by))


def on_device(interaction, amplitudes, driver, dressing, occ_energy, vir_energy):
    row, col = lax.axis_index("row"), lax.axis_index("col")
    zh, y = row // 4, row % 4
    zl, x, k = col // 8, (col // 2) % 4, col % 2
    size = driver.shape[0]
    half = size // 2

    row_line = jnp.tile(vir_energy.reshape(2, size), (1, 1))
    row_energy = occ_energy[row // 2] - lax.dynamic_index_in_dim(row_line, row % 2, 0, False)
    column_energy = occ_energy[col // 2] - lax.dynamic_index_in_dim(row_line, col % 2, 0, False)

    w0 = interaction
    w1 = send(w0, low=1)
    l0, r0 = send(w0, dx=1), send(w0, dx=-1)
    l1, r1 = send(w1, dx=1), send(w1, dx=-1)
    far0, far1 = send(l0, dx=1), send(r1, dx=-1)
    mine = [
        (0, 0, w0), (1, 0, w1),
        (0, -1, l0), (0, 1, r0),
        (1, -1, l1), (1, 1, r1),
        (0, 2, far0), (1, 2, far1),
    ]
    panel = jnp.zeros((16, size, size), interaction.dtype)

    def place(panel, block, low, dx, core):
        spot = ((zl + low) % 2) * 8 + ((x + dx) % 4) * 2 + (k + core) % 2
        return lax.dynamic_update_slice(panel, block[None], (spot, 0, 0))

    for low, dx, block in mine:
        panel = place(panel, block, low, dx, 0)
        panel = place(panel, send(block, core=1), low, dx, 1)

    t0 = amplitudes
    top, bottom = t0[:half], t0[half:]
    a_top, b_bottom = send(top, high=1), send(bottom, high=-1)
    a_bottom, b_top = send(bottom, high=1), send(top, high=-1)
    c_top, c_bottom = send(a_top, high=1), send(b_bottom, high=-1)
    pieces = [(0, -1, 0, a_top), (half, 1, 0, b_bottom), (half, -1, 0, a_bottom), (0, 1, 0, b_top), (0, 2, 0, c_top), (half, 2, 0, c_bottom)]
    done = [(0, 0, 0, t0)]
    lo, hi = send(t0, dy=1), send(t0, dy=-1)
    done += [(0, 0, -1, lo), (0, 0, 1, hi)]
    done += [(0, 0, 2, send(lo[:half], dy=1)), (half, 0, 2, send(hi[half:], dy=-1))]
    for first, second in ((0, 1), (2, 3), (4, 5)):
        for i, (at, dz, _, block) in enumerate((pieces[first], pieces[second])):
            done.append((at, dz, 0, block))
            lo, hi = send(block, dy=1), send(block, dy=-1)
            done += [(at, dz, -1, lo), (at, dz, 1, hi)]
            far = send(lo, dy=1) if i == 0 else send(hi, dy=-1)
            done.append((at, dz, 2, far))

    total = jnp.zeros((size, size), jnp.float32)
    for at, dz, dy, block in done:
        spot = ((zh + dz) % 4) * 4 + (y + dy) % 4
        left = lax.dynamic_slice(panel, (spot, 0, at), (1, size, block.shape[0]))[0]
        total = total + jnp.dot(left, block, preferred_element_type=jnp.float32)

    denominator = row_energy[:, None] + column_energy[None, :]
    summed = driver.astype(jnp.float32) + total
    first_order = (summed / denominator).astype(jnp.bfloat16)
    other = send(first_order, core=1)
    near = lax.dynamic_slice(dressing, (k * size, k * size), (size, size))
    away = lax.dynamic_slice(dressing, ((1 - k) * size, k * size), (size, size))
    dressed = jnp.dot(first_order, near, preferred_element_type=jnp.float32)
    dressed = dressed + jnp.dot(other, away, preferred_element_type=jnp.float32)
    dressed = dressed.astype(jnp.bfloat16)
    return (summed + dressed.astype(jnp.float32)) / denominator


def solution(mesh):
    return jax.shard_map(
        on_device,
        mesh=mesh,
        in_specs=(P("row", "col"), P("row", "col"), P("row", "col"), P(), P(), P()),
        out_specs=P("row", "col"),
        check_vma=False,
    )
```

```python
import jax
import jax.numpy as jnp
from jax import lax
from jax.experimental import pallas as pl
from jax.experimental.pallas import tpu as pltpu
from jax.sharding import PartitionSpec as P

AXES = ("row", "col")
OWN, NEAR, FAR, OPPOSITE = 0, 1, 2, 3


def device_index(x, y, high, low, core):
    return ((high % 4) * 4 + y % 4) * 16 + (low % 2) * 8 + (x % 4) * 2 + core % 2


def permutation(move):
    pairs = []
    for x in range(4):
        for y in range(4):
            for zh in range(4):
                for zl in range(2):
                    for k in range(2):
                        pairs.append((device_index(x, y, zh, zl, k), device_index(*move(x, y, zh, zl, k))))
    return pairs


FORWARD_X = permutation(lambda x, y, zh, zl, k: (x + 1 - 2 * k, y, zh, zl, k))
FORWARD_Y = permutation(lambda x, y, zh, zl, k: (x, y + 1 - 2 * k, zh, zl, k))
FORWARD_Z = permutation(lambda x, y, zh, zl, k: (x, y, zh + 1 - 2 * k, zl, k))
PARITY = permutation(lambda x, y, zh, zl, k: (x, y, zh, zl + 1, k))
CORES = permutation(lambda x, y, zh, zl, k: (x, y, zh, zl, k + 1))


def send(block, pairs):
    return lax.ppermute(block, AXES, pairs)


def after(block, *earlier):
    return lax.optimization_barrier((block, *earlier))[0]


def accumulate(spots, lefts, rights, wanted, total):
    count, size = len(rights), rights[0].shape[0]
    slots = jnp.full((len(lefts),), -1, jnp.int32)
    for slot, spot in enumerate(wanted):
        slots = jnp.where(spots == spot, slot, slots)

    def kernel(slots_ref, *refs):
        left_refs = refs[: len(lefts)]
        right_refs = refs[len(lefts) : len(lefts) + count]
        rest = refs[len(lefts) + count :]
        total_ref, (out_ref, left_buf, right_buf, left_sem, right_sem) = (None, rest) if total is None else (rest[0], rest[1:])
        for i, ref in enumerate(left_refs):
            slot = slots_ref[i]

            @pl.when(slot >= 0)
            def _(ref=ref, slot=slot):
                pltpu.make_async_copy(ref, left_buf.at[slot], left_sem.at[slot]).start()

        for j, ref in enumerate(right_refs):
            pltpu.make_async_copy(ref, right_buf.at[j], right_sem.at[j]).start()
        if total_ref is None:
            out_ref[...] = jnp.zeros_like(out_ref)
        else:
            out_ref[...] = total_ref[...]

        def step(j, _):
            pltpu.make_async_copy(left_refs[0], left_buf.at[j], left_sem.at[j]).wait()
            pltpu.make_async_copy(right_refs[0], right_buf.at[j], right_sem.at[j]).wait()
            out_ref[...] += jnp.dot(left_buf[j], right_buf[j], preferred_element_type=jnp.float32)
            return 0

        lax.fori_loop(0, count, step, 0)

    whole = pl.BlockSpec(memory_space=pltpu.VMEM)
    anywhere = pl.BlockSpec(memory_space=pl.ANY)
    extra = [] if total is None else [total]
    return pl.pallas_call(
        kernel,
        out_shape=jax.ShapeDtypeStruct((size, size), jnp.float32),
        in_specs=[pl.BlockSpec(memory_space=pltpu.SMEM)] + [anywhere] * (len(lefts) + count) + [whole] * len(extra),
        out_specs=whole,
        scratch_shapes=[
            pltpu.VMEM((count, size, size), jnp.bfloat16),
            pltpu.VMEM((count, size, size), jnp.bfloat16),
            pltpu.SemaphoreType.DMA((count,)),
            pltpu.SemaphoreType.DMA((count,)),
        ],
        compiler_params=pltpu.CompilerParams(vmem_limit_bytes=24 << 20),
        cost_estimate=pl.CostEstimate(flops=2 * count * size**3, bytes_accessed=4 * count * size**2, transcendentals=0),
        name=f"accumulate_{count}",
    )(slots, *lefts, *rights, *extra)


def on_device(interaction, amplitudes, driver, dressing, occ_energy, vir_energy):
    row, col = lax.axis_index("row"), lax.axis_index("col")
    zh, y = row // 4, row % 4
    zl, x, k = col // 8, (col // 2) % 4, col % 2
    sign = 1 - 2 * k
    size = driver.shape[0]

    u0 = amplitudes
    yu = send(u0, FORWARD_Y)
    zu = send(u0, FORWARD_Z)
    v0 = send(u0, CORES)
    yv = send(v0, FORWARD_Y)
    w0 = interaction
    x0 = send(w0, FORWARD_X)
    wv0 = send(w0, CORES)
    xv0 = send(wv0, FORWARD_X)
    y_far = send(after(yu, yv), FORWARD_Y)
    xf0 = send(after(x0, xv0), FORWARD_X)

    w1 = send(after(w0, zu), PARITY)
    zv = send(after(v0, zu), FORWARD_Z)
    zuo = send(zu, CORES)
    n_u = send(after(zu, yv), FORWARD_Y)
    n_v = send(after(zuo, y_far), FORWARD_Y)
    n_far = send(after(n_u, n_u), FORWARD_Y)
    zf = send(after(zu, zv), FORWARD_Z)
    zo = send(zv, CORES)

    x1 = send(after(w1, xf0), FORWARD_X)
    wv1 = send(w1, CORES)
    xv1 = send(wv1, FORWARD_X)
    xf1 = send(after(x1, xv1), FORWARD_X)

    o_v = send(after(zv, n_v), FORWARD_Y)
    o_u = send(after(zo, n_far), FORWARD_Y)
    o_far = send(after(o_u, o_v), FORWARD_Y)
    zfo = send(zf, CORES)
    f_u = send(after(zf, o_u), FORWARD_Y)
    f_v = send(after(zfo, o_far), FORWARD_Y)
    f_far = send(after(f_u, f_u), FORWARD_Y)

    lefts, spots = [], []

    def place(block, dx, low, core):
        where_x = (x - sign * dx) % 4
        contraction = ((zl + low) % 2) * 8 + where_x * 2 + (k + core) % 2
        z_step = (sign * (zh - contraction // 4)) % 4
        y_step = (sign * (y - contraction % 4)) % 4
        lefts.append(block)
        spots.append(z_step * 4 + y_step)

    for low, mine, other, near, near_other, far in ((0, w0, wv0, x0, xv0, xf0), (1, w1, wv1, x1, xv1, xf1)):
        place(mine, OWN, low, 0)
        place(other, OWN, low, 1)
        place(near, NEAR, low, 0)
        place(near_other, NEAR, low, 1)
        place(far, FAR, low, 0)
        place(send(near, CORES), OPPOSITE, low, 1)
        place(send(near_other, CORES), OPPOSITE, low, 0)
        place(send(far, CORES), FAR, low, 1)
    spots = jnp.stack(spots).astype(jnp.int32)

    swap = lambda block: send(block, CORES)
    total = accumulate(
        spots, lefts, [u0, yu, y_far, swap(yv), zu, n_u, n_far, swap(n_v)], [0, 1, 2, 3, 4, 5, 6, 7], None
    )
    total = accumulate(spots, lefts, [zo, o_u, swap(o_v), o_far, zf, f_u], [12, 13, 15, 14, 8, 9], total)
    total = accumulate(spots, lefts, [swap(f_v), f_far], [11, 10], total)

    virtual = vir_energy.reshape(2, size)
    row_energy = occ_energy[row // 2] - lax.dynamic_index_in_dim(virtual, row % 2, 0, False)
    column_energy = occ_energy[col // 2] - lax.dynamic_index_in_dim(virtual, col % 2, 0, False)
    denominator = row_energy[:, None] + column_energy[None, :]
    summed = driver.astype(jnp.float32) + total
    first_order = (summed / denominator).astype(jnp.bfloat16)
    other = send(first_order, CORES)
    mine = lax.dynamic_slice(dressing, (k * size, k * size), (size, size))
    theirs = lax.dynamic_slice(dressing, ((1 - k) * size, k * size), (size, size))
    dressed = jnp.dot(first_order, mine, preferred_element_type=jnp.float32)
    dressed = dressed + jnp.dot(other, theirs, preferred_element_type=jnp.float32)
    dressed = dressed.astype(jnp.bfloat16)
    return (summed + dressed.astype(jnp.float32)) / denominator


def solution(mesh):
    return jax.shard_map(
        on_device,
        mesh=mesh,
        in_specs=(P("row", "col"), P("row", "col"), P("row", "col"), P(), P(), P()),
        out_specs=P("row", "col"),
        check_vma=False,
    )
```

```python
import jax
import jax.numpy as jnp
from jax import lax
from jax.experimental import pallas as pl
from jax.experimental.pallas import tpu as pltpu
from jax.sharding import PartitionSpec as P

AXES = ("row", "col")
OWN, NEAR, FAR, OPPOSITE = 0, 1, 2, 3


def device_index(x, y, high, low, core):
    return ((high % 4) * 4 + y % 4) * 16 + (low % 2) * 8 + (x % 4) * 2 + core % 2


def permutation(move):
    pairs = []
    for x in range(4):
        for y in range(4):
            for zh in range(4):
                for zl in range(2):
                    for k in range(2):
                        pairs.append((device_index(x, y, zh, zl, k), device_index(*move(x, y, zh, zl, k))))
    return pairs


FORWARD_X = permutation(lambda x, y, zh, zl, k: (x + 1 - 2 * k, y, zh, zl, k))
FORWARD_Y = permutation(lambda x, y, zh, zl, k: (x, y + 1 - 2 * k, zh, zl, k))
FORWARD_Z = permutation(lambda x, y, zh, zl, k: (x, y, zh + 1 - 2 * k, zl, k))
PARITY = permutation(lambda x, y, zh, zl, k: (x, y, zh, zl + 1, k))
CORES = permutation(lambda x, y, zh, zl, k: (x, y, zh, zl, k + 1))


def send(block, pairs):
    return lax.ppermute(block, AXES, pairs)


def after(block, *earlier):
    return lax.optimization_barrier((block, *earlier))[0]


MIB = 1 << 20
VMEM = pl.BlockSpec(memory_space=pltpu.VMEM)
ANY = pl.BlockSpec(memory_space=pl.ANY)
HBM = pl.BlockSpec(memory_space=pltpu.HBM)


def place_of_device():
    row, col = lax.axis_index("row"), lax.axis_index("col")
    return (row >> 2) & 3, row & 3, (col >> 3) & 1, (col >> 1) & 3, col & 1


def gray(step):
    return step ^ (step >> 1)


def spot_of(block):
    dx, low, core = block
    zh, y, zl, x, k = place_of_device()
    sign = 1 - 2 * k
    contraction = (((zl + low) & 1) << 3) + (((x - sign * dx) & 3) << 1) + ((k + core) & 1)
    z_step = (sign * (zh - (contraction >> 2))) & 3
    y_step = (sign * (y - (contraction & 3))) & 3
    return gray(z_step) * 4 + gray(y_step)


def start_copies(places, first, lefts, rights, left_buf, right_buf, left_sem, right_sem):
    count = len(rights)
    for ref, block in zip(lefts, places, strict=True):
        slot = spot_of(block) - first

        @pl.when((slot >= 0) & (slot < count))
        def _(ref=ref, slot=slot):
            pltpu.make_async_copy(ref, left_buf.at[slot], left_sem.at[slot]).start()

    for j, ref in enumerate(rights):
        pltpu.make_async_copy(ref, right_buf.at[j], right_sem.at[j]).start()


def add_products(count, left, right, total, left_buf, right_buf, left_sem, right_sem):
    def step(j, _):
        pltpu.make_async_copy(left, left_buf.at[j], left_sem.at[j]).wait()
        pltpu.make_async_copy(right, right_buf.at[j], right_sem.at[j]).wait()
        total[...] += jnp.dot(left_buf[j], right_buf[j], preferred_element_type=jnp.float32)
        return 0

    lax.fori_loop(0, count, step, 0)


def left_specs(lefts):
    return [HBM] + [ANY] * (len(lefts) - 1)


def scratch(count, size):
    return [
        pltpu.VMEM((count, size, size), jnp.bfloat16),
        pltpu.VMEM((count, size, size), jnp.bfloat16),
        pltpu.SemaphoreType.DMA((count,)),
        pltpu.SemaphoreType.DMA((count,)),
    ]


def cost(count, size):
    return pl.CostEstimate(flops=2 * count * size**3, bytes_accessed=4 * count * size**2, transcendentals=0)


def open_sum(places, lefts, rights, driver, occ_energy, vir_energy):
    count, size = len(rights), driver.shape[0]

    def kernel(*refs):
        left_refs, refs = refs[: len(lefts)], refs[len(lefts) :]
        right_refs, refs = refs[:count], refs[count:]
        driver_ref, occ_hbm, vir_hbm, total_ref, denominator_ref, *buffers, driver_buf, occ_ref, vir_ref, sems = refs
        inputs = ((occ_hbm, occ_ref), (vir_hbm, vir_ref), (driver_ref, driver_buf))
        copies = [pltpu.make_async_copy(a, b, sems.at[i]) for i, (a, b) in enumerate(inputs)]
        for copy in copies:
            copy.start()
        start_copies(places, 0, left_refs, right_refs, *buffers)
        for copy in copies:
            copy.wait()
        row, col = lax.axis_index("row"), lax.axis_index("col")

        def line(index):
            parts = [vir_ref[pl.ds((index & 1) * (size // 128) + i, 1), :] for i in range(size // 128)]
            return occ_ref[index >> 1] - jnp.concatenate(parts, axis=1)

        down = jnp.broadcast_to(line(row), (128, size)).T
        across = line(col)
        for i in range(size // 128):
            lanes = slice(i * 128, (i + 1) * 128)
            denominator_ref[:, lanes] = down + across[:, lanes]
        total_ref[...] = driver_buf[...].astype(jnp.float32)
        add_products(count, left_refs[0], right_refs[0], total_ref, *buffers)

    square = jax.ShapeDtypeStruct((size, size), jnp.float32)
    return pl.pallas_call(
        kernel,
        out_shape=(square, square),
        in_specs=left_specs(lefts) + [HBM] + [ANY] * (count - 1) + [HBM] * 3,
        out_specs=(VMEM, VMEM),
        scratch_shapes=scratch(count, size)
        + [
            pltpu.VMEM((size, size), driver.dtype),
            pltpu.SMEM(occ_energy.shape, jnp.float32),
            pltpu.VMEM((vir_energy.shape[0] // 128, 128), jnp.float32),
            pltpu.SemaphoreType.DMA((3,)),
        ],
        compiler_params=pltpu.CompilerParams(vmem_limit_bytes=24 * MIB),
        cost_estimate=cost(count, size),
        name="open_sum",
    )(*lefts, *rights, driver, occ_energy, vir_energy.reshape(-1, 128))


def grow_sum(places, first, lefts, rights, total):
    count, size = len(rights), total.shape[0]

    def kernel(*refs):
        left_refs, refs = refs[: len(lefts)], refs[len(lefts) :]
        right_refs, refs = refs[:count], refs[count:]
        total_ref, out_ref, *buffers = refs
        start_copies(places, first, left_refs, right_refs, *buffers)
        out_ref[...] = total_ref[...]
        add_products(count, left_refs[0], right_refs[0], out_ref, *buffers)

    return pl.pallas_call(
        kernel,
        out_shape=jax.ShapeDtypeStruct((size, size), jnp.float32),
        in_specs=left_specs(lefts) + [ANY] * count + [VMEM],
        out_specs=VMEM,
        scratch_shapes=scratch(count, size),
        compiler_params=pltpu.CompilerParams(vmem_limit_bytes=24 * MIB),
        cost_estimate=cost(count, size),
        name="grow_sum",
    )(*lefts, *rights, total)


def close_sum(places, first, lefts, rights, total, denominator):
    count, size = len(rights), total.shape[0]

    def kernel(*refs):
        left_refs, refs = refs[: len(lefts)], refs[len(lefts) :]
        right_refs, refs = refs[:count], refs[count:]
        total_ref, denominator_ref, out_ref, first_ref, *buffers = refs
        start_copies(places, first, left_refs, right_refs, *buffers)
        out_ref[...] = total_ref[...]
        add_products(count, left_refs[0], right_refs[0], out_ref, *buffers)
        first_ref[...] = (out_ref[...] / denominator_ref[...]).astype(jnp.bfloat16)

    return pl.pallas_call(
        kernel,
        out_shape=(jax.ShapeDtypeStruct((size, size), jnp.float32), jax.ShapeDtypeStruct((size, size), jnp.bfloat16)),
        in_specs=left_specs(lefts) + [ANY] * count + [VMEM, VMEM],
        out_specs=(VMEM, VMEM),
        scratch_shapes=scratch(count, size),
        compiler_params=pltpu.CompilerParams(vmem_limit_bytes=24 * MIB),
        cost_estimate=cost(count, size),
        name="close_sum",
    )(*lefts, *rights, total, denominator)


def quadrant(dressing_ref, size, up):
    core = lax.axis_index("col") & 1
    rows = pl.ds(pl.multiple_of((core ^ up) * size, size), size)
    columns = pl.ds(pl.multiple_of(core * size, size), size)
    return dressing_ref[rows, columns]


def dress_mine(first_order, dressing):
    size = first_order.shape[0]

    def kernel(first_ref, dressing_ref, out_ref):
        out_ref[...] = jnp.dot(first_ref[...], quadrant(dressing_ref, size, 0), preferred_element_type=jnp.float32)

    return pl.pallas_call(
        kernel,
        out_shape=jax.ShapeDtypeStruct((size, size), jnp.float32),
        in_specs=[VMEM, VMEM],
        out_specs=VMEM,
        compiler_params=pltpu.CompilerParams(vmem_limit_bytes=16 * MIB),
        cost_estimate=cost(1, size),
        name="dress_mine",
    )(first_order, dressing)


def finish(part, other, dressing, summed, denominator):
    size = summed.shape[0]

    def kernel(part_ref, other_ref, dressing_ref, summed_ref, denominator_ref, out_ref):
        dressed = part_ref[...] + jnp.dot(other_ref[...], quadrant(dressing_ref, size, 1), preferred_element_type=jnp.float32)
        dressed = dressed.astype(jnp.bfloat16).astype(jnp.float32)
        out_ref[...] = (summed_ref[...] + dressed) / denominator_ref[...]

    return pl.pallas_call(
        kernel,
        out_shape=jax.ShapeDtypeStruct((size, size), jnp.float32),
        in_specs=[VMEM] * 5,
        out_specs=VMEM,
        compiler_params=pltpu.CompilerParams(vmem_limit_bytes=24 * MIB),
        cost_estimate=cost(1, size),
        name="finish",
    )(part, other, dressing, summed, denominator)


def on_device(interaction, amplitudes, driver, dressing, occ_energy, vir_energy):
    u0, w0 = amplitudes, interaction
    v0 = send(u0, CORES)
    yu = send(u0, FORWARD_Y)
    zu = send(u0, FORWARD_Z)
    w1 = send(w0, PARITY)
    wv0 = send(w0, CORES)
    x0 = send(w0, FORWARD_X)
    yv = send(v0, FORWARD_Y)
    xv0 = send(wv0, FORWARD_X)
    y_far = send(yu, FORWARD_Y)
    xf0 = send(x0, FORWARD_X)

    zv = send(after(v0, zu), FORWARD_Z)
    zuo = send(zu, CORES)
    n_u = send(after(zu, yv), FORWARD_Y)
    x1 = send(after(w1, xv0), FORWARD_X)
    wv1 = send(w1, CORES)
    n_v = send(after(zuo, y_far), FORWARD_Y)
    xv1 = send(after(wv1, xf0), FORWARD_X)
    n_far = send(n_u, FORWARD_Y)
    xf1 = send(x1, FORWARD_X)
    zf = send(after(zu, zv), FORWARD_Z)
    zo = send(zv, CORES)
    o_v = send(after(zv, n_v), FORWARD_Y)
    o_u = send(after(zo, n_far), FORWARD_Y)
    o_far = send(after(o_u, o_v), FORWARD_Y)
    zfo = send(zf, CORES)

    swap = lambda block: send(block, CORES)
    lefts, places = [], []
    for low, mine, other, near, near_other, far in ((0, w0, wv0, x0, xv0, xf0), (1, w1, wv1, x1, xv1, xf1)):
        lefts += [mine, other, near, near_other, far, swap(near), swap(near_other), swap(far)]
        steps = [(OWN, 0), (OWN, 1), (NEAR, 0), (NEAR, 1), (FAR, 0), (OPPOSITE, 1), (OPPOSITE, 0), (FAR, 1)]
        places += [(dx, low, core) for dx, core in steps]

    early = [u0, yu, swap(yv), y_far, zu, n_u, swap(n_v), n_far]
    total, denominator = open_sum(places, lefts, early, driver, occ_energy, vir_energy)
    f_u = send(after(zf, o_u, total), FORWARD_Y)
    f_v = send(after(zfo, o_far), FORWARD_Y)
    f_far = send(f_u, FORWARD_Y)
    total = grow_sum(places, 8, lefts, [zo, o_u, swap(o_v), o_far, zf, f_u], total)
    summed, first_order = close_sum(places, 14, lefts, [swap(f_v), f_far], total, denominator)
    other = send(first_order, CORES)
    part = dress_mine(first_order, dressing)
    return finish(part, other, dressing, summed, denominator)


def solution(mesh):
    return jax.shard_map(
        on_device,
        mesh=mesh,
        in_specs=(P("row", "col"), P("row", "col"), P("row", "col"), P(), P(), P()),
        out_specs=P("row", "col"),
        check_vma=False,
    )
```

```python
import jax
import jax.numpy as jnp
from jax import lax
from jax.experimental import pallas as pl
from jax.experimental.pallas import tpu as pltpu
from jax.sharding import PartitionSpec as P


AXES = ("row", "col")
OWN, NEAR, FAR, OPPOSITE = 0, 1, 2, 3


def device_index(x, y, high, low, core):
    return ((high % 4) * 4 + y % 4) * 16 + (low % 2) * 8 + (x % 4) * 2 + core % 2


def permutation(move):
    pairs = []
    for x in range(4):
        for y in range(4):
            for zh in range(4):
                for zl in range(2):
                    for k in range(2):
                        pairs.append((device_index(x, y, zh, zl, k), device_index(*move(x, y, zh, zl, k))))
    return pairs


FORWARD_X = permutation(lambda x, y, zh, zl, k: (x + 1 - 2 * k, y, zh, zl, k))
FORWARD_Y = permutation(lambda x, y, zh, zl, k: (x, y + 1 - 2 * k, zh, zl, k))
FORWARD_Z = permutation(lambda x, y, zh, zl, k: (x, y, zh + 1 - 2 * k, zl, k))
PARITY = permutation(lambda x, y, zh, zl, k: (x, y, zh, zl + 1, k))
CORES = permutation(lambda x, y, zh, zl, k: (x, y, zh, zl, k + 1))


def send(block, pairs):
    return lax.ppermute(block, AXES, pairs)


MIB = 1 << 20
VMEM = pl.BlockSpec(memory_space=pltpu.VMEM)
ANY = pl.BlockSpec(memory_space=pl.ANY)


def place_of_device():
    row, col = lax.axis_index("row"), lax.axis_index("col")
    return (row >> 2) & 3, row & 3, (col >> 3) & 1, (col >> 1) & 3, col & 1


def gray(step):
    return step ^ (step >> 1)


def spot_of(block):
    dx, low, core = block
    zh, y, zl, x, k = place_of_device()
    sign = 1 - 2 * k
    contraction = (((zl + low) & 1) << 3) + (((x - sign * dx) & 3) << 1) + ((k + core) & 1)
    z_step = (sign * (zh - (contraction >> 2))) & 3
    y_step = (sign * (y - (contraction & 3))) & 3
    return gray(z_step) * 4 + gray(y_step)


LAST = (13, 14, 15)
FINAL = 13
BEFORE = tuple(spot for spot in range(16) if spot not in LAST)
LATE_BLOCKS = ((FAR, 1, 0), (FAR, 1, 1), (NEAR, 1, 1), (OPPOSITE, 1, 0))
SOON = tuple(range(9))
FIRST_BLOCKS = tuple((dx, 0, core) for dx in (OWN, NEAR, FAR, OPPOSITE) for core in (0, 1))


def first_mask():
    mask = jnp.int32(0)
    for block in FIRST_BLOCKS:
        mask = mask | (jnp.int32(1) << spot_of(block))
    return mask & sum(1 << spot for spot in SOON)


def early_mask():
    mask = jnp.int32(sum(1 << spot for spot in BEFORE))
    for block in LATE_BLOCKS:
        mask = mask & ~(jnp.int32(1) << spot_of(block))
    return mask & ~first_mask()


def middle_mask():
    return early_mask() ^ first_mask() ^ (0xFFFF - (1 << FINAL))


def final_mask():
    return jnp.int32(1 << FINAL)


def has(mask, spot):
    return ((mask >> spot) & 1) == 1


def add_products(mask, places, spots, lefts, rights, total, ranks, left_buf, right_buf, left_sem, right_sem):
    size = total.shape[0]
    count = jnp.int32(0)
    for spot in range(16):
        ranks[spot] = count
        count = count + ((mask >> spot) & 1)

    def part(rank):
        return pl.ds(pl.multiple_of((rank & 1) * size, size), size)

    def left_copy(ref, rank):
        return pltpu.make_async_copy(ref, left_buf.at[rank >> 1, :, part(rank)], left_sem.at[rank])

    def right_copy(ref, rank):
        return pltpu.make_async_copy(ref, right_buf.at[rank >> 1, part(rank), :], right_sem.at[rank])

    for ref, block in zip(lefts, places, strict=True):
        spot = spot_of(block)

        @pl.when(has(mask, spot))
        def _(ref=ref, spot=spot):
            left_copy(ref, ranks[spot]).start()

    for ref, spot in zip(rights, spots, strict=True):

        @pl.when(has(mask, spot))
        def _(ref=ref, spot=spot):
            right_copy(ref, ranks[spot]).start()

    def arrive(rank):
        left_copy(lefts[0], rank).wait()
        right_copy(rights[0], rank).wait()

    def step(pair, _):
        arrive(2 * pair)
        arrive(2 * pair + 1)
        total[...] += jnp.dot(left_buf[pair], right_buf[pair], preferred_element_type=jnp.float32)
        return 0

    lax.fori_loop(0, count >> 1, step, 0)

    @pl.when((count & 1) == 1)
    def _():
        pair = count >> 1
        arrive(2 * pair)
        total[...] += jnp.dot(left_buf[pair, :, :size], right_buf[pair, :size, :], preferred_element_type=jnp.float32)


def scratch(count, size):
    pairs = (count + 1) // 2
    return [
        pltpu.SMEM((16,), jnp.int32),
        pltpu.VMEM((pairs, size, 2 * size), jnp.bfloat16),
        pltpu.VMEM((pairs, 2 * size, size), jnp.bfloat16),
        pltpu.SemaphoreType.DMA((2 * pairs,)),
        pltpu.SemaphoreType.DMA((2 * pairs,)),
    ]


def cost(count, size):
    return pl.CostEstimate(flops=2 * count * size**3, bytes_accessed=4 * count * size**2, transcendentals=0)


def energies(occ_energy, vir_energy, size):
    def kernel(occ_hbm, vir_hbm, denominator_ref, occ_ref, vir_ref, sems):
        moves = ((occ_hbm, occ_ref), (vir_hbm, vir_ref))
        copies = [pltpu.make_async_copy(a, b, sems.at[i]) for i, (a, b) in enumerate(moves)]
        for copy in copies:
            copy.start()
        for copy in copies:
            copy.wait()
        row, col = lax.axis_index("row"), lax.axis_index("col")

        def line(index):
            parts = [vir_ref[pl.ds((index & 1) * (size // 128) + i, 1), :] for i in range(size // 128)]
            return occ_ref[index >> 1] - jnp.concatenate(parts, axis=1)

        down = jnp.broadcast_to(line(row), (128, size)).T
        across = line(col)
        for i in range(size // 128):
            lanes = slice(i * 128, (i + 1) * 128)
            denominator_ref[:, lanes] = down + across[:, lanes]

    return pl.pallas_call(
        kernel,
        out_shape=jax.ShapeDtypeStruct((size, size), jnp.float32),
        in_specs=[ANY] * 2,
        out_specs=VMEM,
        scratch_shapes=[
            pltpu.SMEM(occ_energy.shape, jnp.float32),
            pltpu.VMEM((vir_energy.shape[0] // 128, 128), jnp.float32),
            pltpu.SemaphoreType.DMA((2,)),
        ],
        compiler_params=pltpu.CompilerParams(vmem_limit_bytes=8 * MIB),
        cost_estimate=pl.CostEstimate(flops=20_000_000_000, bytes_accessed=0, transcendentals=0),
        name="energies",
    )(occ_energy, vir_energy.reshape(-1, 128))


def prepare(interaction, amplitudes, driver):
    size = driver.shape[0]

    def kernel(w_hbm, u_hbm, driver_hbm, w_ref, u_ref, total_ref, driver_ref, sems):
        moves = ((driver_hbm, driver_ref), (w_hbm, w_ref), (u_hbm, u_ref))
        copies = [pltpu.make_async_copy(a, b, sems.at[i]) for i, (a, b) in enumerate(moves)]
        for copy in copies:
            copy.start()
        copies[0].wait()
        total_ref[...] = driver_ref[...].astype(jnp.float32)
        for copy in copies[1:]:
            copy.wait()

    block = jax.ShapeDtypeStruct((size, size), jnp.bfloat16)
    return pl.pallas_call(
        kernel,
        out_shape=(block, block, jax.ShapeDtypeStruct((size, size), jnp.float32)),
        in_specs=[ANY] * 3,
        out_specs=(VMEM,) * 3,
        scratch_shapes=[pltpu.VMEM((size, size), driver.dtype), pltpu.SemaphoreType.DMA((3,))],
        compiler_params=pltpu.CompilerParams(vmem_limit_bytes=8 * MIB),
        cost_estimate=pl.CostEstimate(flops=2 * size**2, bytes_accessed=12 * size**2, transcendentals=0),
        name="prepare",
    )(interaction, amplitudes, driver)


def grow_sum(mask, room, places, spots, lefts, rights, total):
    count, size = len(rights), total.shape[0]

    def kernel(*refs):
        left_refs, refs = refs[: len(lefts)], refs[len(lefts) :]
        right_refs, refs = refs[:count], refs[count:]
        total_ref, out_ref, *buffers = refs
        out_ref[...] = total_ref[...]
        add_products(mask(), places, spots, left_refs, right_refs, out_ref, *buffers)

    return pl.pallas_call(
        kernel,
        out_shape=jax.ShapeDtypeStruct((size, size), jnp.float32),
        in_specs=[ANY] * (len(lefts) + count) + [VMEM],
        out_specs=VMEM,
        scratch_shapes=scratch(room, size),
        compiler_params=pltpu.CompilerParams(vmem_limit_bytes=24 * MIB),
        cost_estimate=cost(room, size),
    )(*lefts, *rights, total)


def close_sum(places, spots, lefts, rights, total, denominator):
    count, size = len(rights), total.shape[0]

    def kernel(*refs):
        left_refs, refs = refs[: len(lefts)], refs[len(lefts) :]
        right_refs, refs = refs[:count], refs[count:]
        total_ref, denominator_ref, out_ref, first_ref, *buffers = refs
        out_ref[...] = total_ref[...]
        add_products(final_mask(), places, spots, left_refs, right_refs, out_ref, *buffers)
        first_ref[...] = (out_ref[...] / denominator_ref[...]).astype(jnp.bfloat16)

    return pl.pallas_call(
        kernel,
        out_shape=(jax.ShapeDtypeStruct((size, size), jnp.float32), jax.ShapeDtypeStruct((size, size), jnp.bfloat16)),
        in_specs=[ANY] * (len(lefts) + count) + [VMEM, VMEM],
        out_specs=(VMEM, VMEM),
        scratch_shapes=scratch(1, size),
        compiler_params=pltpu.CompilerParams(vmem_limit_bytes=24 * MIB),
        cost_estimate=cost(1, size),
        name="close_sum",
    )(*lefts, *rights, total, denominator)


def quadrant(dressing_ref, size, up):
    core = lax.axis_index("col") & 1
    rows = pl.ds(pl.multiple_of((core ^ up) * size, size), size)
    columns = pl.ds(pl.multiple_of(core * size, size), size)
    return dressing_ref[rows, columns]


def dress_mine(first_order, dressing):
    size = first_order.shape[0]

    def kernel(first_ref, dressing_ref, out_ref):
        out_ref[...] = jnp.dot(first_ref[...], quadrant(dressing_ref, size, 0), preferred_element_type=jnp.float32)

    return pl.pallas_call(
        kernel,
        out_shape=jax.ShapeDtypeStruct((size, size), jnp.float32),
        in_specs=[VMEM, VMEM],
        out_specs=VMEM,
        compiler_params=pltpu.CompilerParams(vmem_limit_bytes=16 * MIB),
        cost_estimate=cost(1, size),
        name="dress_mine",
    )(first_order, dressing)


def finish(part, other, dressing, summed, denominator):
    size = summed.shape[0]

    rows = size // 4

    def kernel(part_ref, other_ref, dressing_ref, summed_ref, denominator_ref, out_ref, buf, sems):
        right = quadrant(dressing_ref, size, 1)
        copies = []
        for i in range(4):
            here = slice(i * rows, (i + 1) * rows)
            dressed = part_ref[here] + jnp.dot(other_ref[here], right, preferred_element_type=jnp.float32)
            dressed = dressed.astype(jnp.bfloat16).astype(jnp.float32)
            buf[here] = (summed_ref[here] + dressed) / denominator_ref[here]
            copies.append(pltpu.make_async_copy(buf.at[here], out_ref.at[here], sems.at[i]))
            copies[-1].start()
        for copy in copies:
            copy.wait()

    return pl.pallas_call(
        kernel,
        out_shape=jax.ShapeDtypeStruct((size, size), jnp.float32),
        in_specs=[VMEM] * 5,
        out_specs=ANY,
        scratch_shapes=[pltpu.VMEM((size, size), jnp.float32), pltpu.SemaphoreType.DMA((4,))],
        compiler_params=pltpu.CompilerParams(vmem_limit_bytes=24 * MIB),
        cost_estimate=cost(1, size),
        name="finish",
    )(part, other, dressing, summed, denominator)


def update(interaction, amplitudes, driver, dressing, occ_energy, vir_energy):
    swap = lambda block: send(block, CORES)
    denominator = energies(occ_energy, vir_energy, driver.shape[0])
    w0, u0, total = prepare(interaction, amplitudes, driver)

    v0 = swap(amplitudes)
    yu = send(amplitudes, FORWARD_Y)
    yv = send(v0, FORWARD_Y)
    y_far = send(yu, FORWARD_Y)
    zu = send(amplitudes, FORWARD_Z)
    zv = send(v0, FORWARD_Z)
    zf = send(zu, FORWARD_Z)
    zuo, zo, zfo = swap(zu), swap(zv), swap(zf)
    n_u = send(zu, FORWARD_Y)
    n_v = send(zuo, FORWARD_Y)
    n_far = send(n_u, FORWARD_Y)
    o_v = send(zv, FORWARD_Y)
    o_u = send(zo, FORWARD_Y)
    o_far = send(o_u, FORWARD_Y)
    f_u = send(zf, FORWARD_Y)
    f_v = send(zfo, FORWARD_Y)
    f_far = send(n_far, FORWARD_Z)

    lefts, places = [], []
    w1 = send(interaction, PARITY)
    for low, mine, kept in ((0, interaction, w0), (1, w1, w1)):
        other = swap(mine)
        near = send(mine, FORWARD_X)
        near_other = send(other, FORWARD_X)
        far = send(near, FORWARD_X)
        lefts += [kept, other, near, near_other, far]
        lefts += [swap(near), swap(near_other), swap(far)]
        steps = [(OWN, 0), (OWN, 1), (NEAR, 0), (NEAR, 1), (FAR, 0), (OPPOSITE, 1), (OPPOSITE, 0), (FAR, 1)]
        places += [(dx, low, core) for dx, core in steps]

    rights = [u0, yu, swap(yv), y_far]
    rights += [zu, n_u, swap(n_v), n_far]
    rights += [zo, o_u, swap(o_v), o_far]
    rights += [zf, f_u, swap(f_v), f_far]

    def grow(mask, room, blocks, spots, total):
        chosen = [i for i, block in enumerate(places) if block in blocks]
        return grow_sum(
            mask, room, [places[i] for i in chosen], spots, [lefts[i] for i in chosen], [rights[i] for i in spots], total
        )

    total = grow(first_mask, 8, FIRST_BLOCKS, SOON, total)
    total = grow(early_mask, 9, [block for block in places if block not in LATE_BLOCKS], BEFORE, total)
    total = grow(middle_mask, 6, places, [spot for spot in range(16) if spot != FINAL], total)
    summed, first_order = close_sum(places, (FINAL,), lefts, [rights[FINAL]], total, denominator)
    other = swap(first_order)
    part = dress_mine(first_order, dressing)
    return finish(part, other, dressing, summed, denominator)


def solution(mesh):
    return jax.shard_map(
        update,
        mesh=mesh,
        in_specs=(P("row", "col"), P("row", "col"), P("row", "col"), P(), P(), P()),
        out_specs=P("row", "col"),
        check_vma=False,
    )
```

```python
import jax
import jax.numpy as jnp
from jax import lax
from jax.experimental import pallas as pl
from jax.experimental.pallas import tpu as pltpu
from jax.sharding import PartitionSpec as P


AXES = ("row", "col")
OWN, NEAR, FAR, OPPOSITE = 0, 1, 2, 3


def device_index(x, y, high, low, core):
    return ((high % 4) * 4 + y % 4) * 16 + (low % 2) * 8 + (x % 4) * 2 + core % 2


def permutation(move):
    pairs = []
    for x in range(4):
        for y in range(4):
            for zh in range(4):
                for zl in range(2):
                    for k in range(2):
                        pairs.append((device_index(x, y, zh, zl, k), device_index(*move(x, y, zh, zl, k))))
    return pairs


FORWARD_X = permutation(lambda x, y, zh, zl, k: (x + 1 - 2 * k, y, zh, zl, k))
FORWARD_Y = permutation(lambda x, y, zh, zl, k: (x, y + 1 - 2 * k, zh, zl, k))
FORWARD_Z = permutation(lambda x, y, zh, zl, k: (x, y, zh + 1 - 2 * k, zl, k))
PARITY = permutation(lambda x, y, zh, zl, k: (x, y, zh, zl + 1, k))
CORES = permutation(lambda x, y, zh, zl, k: (x, y, zh, zl, k + 1))


def send(block, pairs):
    return lax.ppermute(block, AXES, pairs)


MIB = 1 << 20
VMEM = pl.BlockSpec(memory_space=pltpu.VMEM)
ANY = pl.BlockSpec(memory_space=pl.ANY)


def place_of_device():
    row, col = lax.axis_index("row"), lax.axis_index("col")
    return (row >> 2) & 3, row & 3, (col >> 3) & 1, (col >> 1) & 3, col & 1


def gray(step):
    return step ^ (step >> 1)


def spot_of(block):
    dx, low, core = block
    zh, y, zl, x, k = place_of_device()
    sign = 1 - 2 * k
    contraction = (((zl + low) & 1) << 3) + (((x - sign * dx) & 3) << 1) + ((k + core) & 1)
    z_step = (sign * (zh - (contraction >> 2))) & 3
    y_step = (sign * (y - (contraction & 3))) & 3
    return gray(z_step) * 4 + gray(y_step)


LAST = (13, 14, 15)
FINAL = 13
BEFORE = tuple(spot for spot in range(16) if spot not in LAST)
LATE_BLOCKS = ((FAR, 1, 0), (FAR, 1, 1), (NEAR, 1, 1), (OPPOSITE, 1, 0))
LAST_BLOCKS = LATE_BLOCKS[:2]
SOON = (0, 1, 2, 3, 4, 5, 8)
FIRST_BLOCKS = tuple((dx, 0, core) for dx in (OWN, NEAR, FAR, OPPOSITE) for core in (0, 1))


def first_mask():
    mask = jnp.int32(0)
    for block in FIRST_BLOCKS:
        mask = mask | (jnp.int32(1) << spot_of(block))
    return mask & sum(1 << spot for spot in SOON)


def early_mask():
    mask = jnp.int32(sum(1 << spot for spot in BEFORE))
    for block in LATE_BLOCKS:
        mask = mask & ~(jnp.int32(1) << spot_of(block))
    return mask & ~first_mask()


def middle_mask():
    return 0xFFFF ^ early_mask() ^ first_mask() ^ last_mask() ^ final_mask()


def last_mask():
    mask = jnp.int32(0)
    for block in LAST_BLOCKS:
        mask = mask | (jnp.int32(1) << spot_of(block))
    return mask & (0xFFFF - (1 << FINAL))


def final_mask():
    return jnp.int32(1 << FINAL)


def has(mask, spot):
    return ((mask >> spot) & 1) == 1


def add_products(mask, places, spots, lefts, rights, total, ranks, left_buf, right_buf, left_sem, right_sem):
    size = total.shape[0]
    count = jnp.int32(0)
    for spot in range(16):
        ranks[spot] = count
        count = count + ((mask >> spot) & 1)

    def part(rank):
        return pl.ds(pl.multiple_of((rank & 1) * size, size), size)

    def left_copy(ref, rank):
        return pltpu.make_async_copy(ref, left_buf.at[rank >> 1, :, part(rank)], left_sem.at[rank])

    def right_copy(ref, rank):
        return pltpu.make_async_copy(ref, right_buf.at[rank >> 1, part(rank), :], right_sem.at[rank])

    for ref, block in zip(lefts, places, strict=True):
        spot = spot_of(block)

        @pl.when(has(mask, spot))
        def _(ref=ref, spot=spot):
            left_copy(ref, ranks[spot]).start()

    for ref, spot in zip(rights, spots, strict=True):

        @pl.when(has(mask, spot))
        def _(ref=ref, spot=spot):
            right_copy(ref, ranks[spot]).start()

    def arrive(rank):
        left_copy(lefts[0], rank).wait()
        right_copy(rights[0], rank).wait()

    def step(pair, _):
        arrive(2 * pair)
        arrive(2 * pair + 1)
        total[...] += jnp.dot(left_buf[pair], right_buf[pair], preferred_element_type=jnp.float32)
        return 0

    lax.fori_loop(0, count >> 1, step, 0)

    @pl.when((count & 1) == 1)
    def _():
        pair = count >> 1
        arrive(2 * pair)
        total[...] += jnp.dot(left_buf[pair, :, :size], right_buf[pair, :size, :], preferred_element_type=jnp.float32)


def scratch(count, size):
    pairs = (count + 1) // 2
    return [
        pltpu.SMEM((16,), jnp.int32),
        pltpu.VMEM((pairs, size, 2 * size), jnp.bfloat16),
        pltpu.VMEM((pairs, 2 * size, size), jnp.bfloat16),
        pltpu.SemaphoreType.DMA((2 * pairs,)),
        pltpu.SemaphoreType.DMA((2 * pairs,)),
    ]


def cost(count, size):
    return pl.CostEstimate(flops=2 * count * size**3, bytes_accessed=4 * count * size**2, transcendentals=0)


def energies(occ_energy, vir_energy, size):
    def kernel(occ_hbm, vir_hbm, inverse_ref, occ_ref, vir_ref, sems):
        moves = ((occ_hbm, occ_ref), (vir_hbm, vir_ref))
        copies = [pltpu.make_async_copy(a, b, sems.at[i]) for i, (a, b) in enumerate(moves)]
        for copy in copies:
            copy.start()
        for copy in copies:
            copy.wait()
        row, col = lax.axis_index("row"), lax.axis_index("col")

        def line(index):
            parts = [vir_ref[pl.ds((index & 1) * (size // 128) + i, 1), :] for i in range(size // 128)]
            return occ_ref[index >> 1] - jnp.concatenate(parts, axis=1)

        down = jnp.broadcast_to(line(row), (128, size)).T
        across = line(col)
        for i in range(size // 128):
            lanes = slice(i * 128, (i + 1) * 128)
            inverse_ref[:, lanes] = 1.0 / (down + across[:, lanes])

    return pl.pallas_call(
        kernel,
        out_shape=jax.ShapeDtypeStruct((size, size), jnp.float32),
        in_specs=[ANY] * 2,
        out_specs=VMEM,
        scratch_shapes=[
            pltpu.SMEM(occ_energy.shape, jnp.float32),
            pltpu.VMEM((vir_energy.shape[0] // 128, 128), jnp.float32),
            pltpu.SemaphoreType.DMA((2,)),
        ],
        compiler_params=pltpu.CompilerParams(vmem_limit_bytes=8 * MIB),
        cost_estimate=pl.CostEstimate(flops=20_000_000_000, bytes_accessed=0, transcendentals=0),
        name="energies",
    )(occ_energy, vir_energy.reshape(-1, 128))


def prepare(interaction, amplitudes, driver):
    size = driver.shape[0]

    def kernel(w_hbm, u_hbm, driver_hbm, w_ref, u_ref, total_ref, driver_ref, sems):
        moves = ((driver_hbm, driver_ref), (w_hbm, w_ref), (u_hbm, u_ref))
        copies = [pltpu.make_async_copy(a, b, sems.at[i]) for i, (a, b) in enumerate(moves)]
        for copy in copies:
            copy.start()
        copies[0].wait()
        total_ref[...] = driver_ref[...].astype(jnp.float32)
        for copy in copies[1:]:
            copy.wait()

    block = jax.ShapeDtypeStruct((size, size), jnp.bfloat16)
    return pl.pallas_call(
        kernel,
        out_shape=(block, block, jax.ShapeDtypeStruct((size, size), jnp.float32)),
        in_specs=[ANY] * 3,
        out_specs=(VMEM,) * 3,
        scratch_shapes=[pltpu.VMEM((size, size), driver.dtype), pltpu.SemaphoreType.DMA((3,))],
        compiler_params=pltpu.CompilerParams(vmem_limit_bytes=8 * MIB),
        cost_estimate=pl.CostEstimate(flops=2 * size**2, bytes_accessed=12 * size**2, transcendentals=0),
        name="prepare",
    )(interaction, amplitudes, driver)


def grow_sum(mask, room, places, spots, lefts, rights, total):
    count, size = len(rights), total.shape[0]

    def kernel(*refs):
        left_refs, refs = refs[: len(lefts)], refs[len(lefts) :]
        right_refs, refs = refs[:count], refs[count:]
        total_ref, out_ref, *buffers = refs
        out_ref[...] = total_ref[...]
        add_products(mask(), places, spots, left_refs, right_refs, out_ref, *buffers)

    return pl.pallas_call(
        kernel,
        out_shape=jax.ShapeDtypeStruct((size, size), jnp.float32),
        in_specs=[ANY] * (len(lefts) + count) + [VMEM],
        out_specs=VMEM,
        scratch_shapes=scratch(room, size),
        compiler_params=pltpu.CompilerParams(vmem_limit_bytes=24 * MIB),
        cost_estimate=cost(room, size),
    )(*lefts, *rights, total)


def close_sum(places, spots, lefts, rights, total, inverse):
    count, size = len(rights), total.shape[0]

    def kernel(*refs):
        left_refs, refs = refs[: len(lefts)], refs[len(lefts) :]
        right_refs, refs = refs[:count], refs[count:]
        total_ref, inverse_ref, out_ref, first_ref, *buffers = refs
        out_ref[...] = total_ref[...]
        add_products(final_mask(), places, spots, left_refs, right_refs, out_ref, *buffers)
        first_ref[...] = (out_ref[...] * inverse_ref[...]).astype(jnp.bfloat16)

    return pl.pallas_call(
        kernel,
        out_shape=(jax.ShapeDtypeStruct((size, size), jnp.float32), jax.ShapeDtypeStruct((size, size), jnp.bfloat16)),
        in_specs=[ANY] * (len(lefts) + count) + [VMEM, VMEM],
        out_specs=(VMEM, VMEM),
        scratch_shapes=scratch(1, size),
        compiler_params=pltpu.CompilerParams(vmem_limit_bytes=24 * MIB),
        cost_estimate=cost(1, size),
        name="close_sum",
    )(*lefts, *rights, total, inverse)


def quadrant(dressing_ref, size, up):
    core = lax.axis_index("col") & 1
    rows = pl.ds(pl.multiple_of((core ^ up) * size, size), size)
    columns = pl.ds(pl.multiple_of(core * size, size), size)
    return dressing_ref[rows, columns]


def dress_mine(first_order, dressing):
    size = first_order.shape[0]

    def kernel(first_ref, dressing_ref, out_ref):
        out_ref[...] = jnp.dot(first_ref[...], quadrant(dressing_ref, size, 0), preferred_element_type=jnp.float32)

    return pl.pallas_call(
        kernel,
        out_shape=jax.ShapeDtypeStruct((size, size), jnp.float32),
        in_specs=[VMEM, VMEM],
        out_specs=VMEM,
        compiler_params=pltpu.CompilerParams(vmem_limit_bytes=16 * MIB),
        cost_estimate=cost(1, size),
        name="dress_mine",
    )(first_order, dressing)


def finish(part, other, dressing, summed, inverse):
    size = summed.shape[0]

    rows = size // 4

    def kernel(part_ref, other_ref, dressing_ref, summed_ref, inverse_ref, out_ref, buf, sems):
        right = quadrant(dressing_ref, size, 1)
        copies = []
        for i in range(4):
            here = slice(i * rows, (i + 1) * rows)
            dressed = part_ref[here] + jnp.dot(other_ref[here], right, preferred_element_type=jnp.float32)
            dressed = dressed.astype(jnp.bfloat16).astype(jnp.float32)
            buf[here] = (summed_ref[here] + dressed) * inverse_ref[here]
            copies.append(pltpu.make_async_copy(buf.at[here], out_ref.at[here], sems.at[i]))
            copies[-1].start()
        for copy in copies:
            copy.wait()

    return pl.pallas_call(
        kernel,
        out_shape=jax.ShapeDtypeStruct((size, size), jnp.float32),
        in_specs=[VMEM] * 5,
        out_specs=ANY,
        scratch_shapes=[pltpu.VMEM((size, size), jnp.float32), pltpu.SemaphoreType.DMA((4,))],
        compiler_params=pltpu.CompilerParams(vmem_limit_bytes=24 * MIB),
        cost_estimate=cost(1, size),
        name="finish",
    )(part, other, dressing, summed, inverse)


def update(interaction, amplitudes, driver, dressing, occ_energy, vir_energy):
    swap = lambda block: send(block, CORES)
    inverse = energies(occ_energy, vir_energy, driver.shape[0])
    w0, u0, total = prepare(interaction, amplitudes, driver)

    v0 = swap(amplitudes)
    yu = send(amplitudes, FORWARD_Y)
    yv = send(v0, FORWARD_Y)
    y_far = send(yu, FORWARD_Y)
    zu = send(amplitudes, FORWARD_Z)
    zv = send(v0, FORWARD_Z)
    zf = send(zu, FORWARD_Z)
    zuo, zo, zfo = swap(zu), swap(zv), swap(zf)
    n_u = send(zu, FORWARD_Y)
    n_v = send(zuo, FORWARD_Y)
    n_far = send(n_u, FORWARD_Y)
    o_v = send(zv, FORWARD_Y)
    o_u = send(zo, FORWARD_Y)
    o_far = send(o_u, FORWARD_Y)
    f_u = send(zf, FORWARD_Y)
    f_v = send(zfo, FORWARD_Y)
    f_far = send(n_far, FORWARD_Z)

    lefts, places = [], []
    w1 = send(interaction, PARITY)
    for low, mine, kept in ((0, interaction, w0), (1, w1, w1)):
        other = swap(mine)
        near = send(mine, FORWARD_X)
        near_other = send(other, FORWARD_X)
        far = send(near, FORWARD_X)
        lefts += [kept, other, near, near_other, far]
        lefts += [swap(near), swap(near_other), swap(far)]
        steps = [(OWN, 0), (OWN, 1), (NEAR, 0), (NEAR, 1), (FAR, 0), (OPPOSITE, 1), (OPPOSITE, 0), (FAR, 1)]
        places += [(dx, low, core) for dx, core in steps]

    rights = [u0, yu, swap(yv), y_far]
    rights += [zu, n_u, swap(n_v), n_far]
    rights += [zo, o_u, swap(o_v), o_far]
    rights += [zf, f_u, swap(f_v), f_far]

    def grow(mask, room, blocks, spots, total):
        chosen = [i for i, block in enumerate(places) if block in blocks]
        return grow_sum(
            mask, room, [places[i] for i in chosen], spots, [lefts[i] for i in chosen], [rights[i] for i in spots], total
        )

    total = grow(first_mask, 8, FIRST_BLOCKS, SOON, total)
    total = grow(early_mask, 10, [block for block in places if block not in LATE_BLOCKS], BEFORE, total)
    most = [spot for spot in range(16) if spot != FINAL]
    total = grow(middle_mask, 4, [block for block in places if block not in LAST_BLOCKS], most, total)
    total = grow(last_mask, 2, LAST_BLOCKS, most, total)
    summed, first_order = close_sum(places, (FINAL,), lefts, [rights[FINAL]], total, inverse)
    other = swap(first_order)
    part = dress_mine(first_order, dressing)
    return finish(part, other, dressing, summed, inverse)


def solution(mesh):
    return jax.shard_map(
        update,
        mesh=mesh,
        in_specs=(P("row", "col"), P("row", "col"), P("row", "col"), P(), P(), P()),
        out_specs=P("row", "col"),
        check_vma=False,
    )
```
